32 devices in a mesh: node: 8 (over z, y), rep: 4 (over x, core).
Axes of the slice: x: 2, y: 2, z: 4, core: 2. Of those that a mesh axis runs over, the one named last changes fastest.
Arguments:
- tokens: bfloat16 [4096, 8192], P(('node', 'rep')), may hold values from -6 to 6
- norm_gain: float32 [8192], replicated, may hold values from 0.5 to 1.5
- key_cotangent: bfloat16 [4096, 512], P(('node', 'rep')), may hold values from -6 to 6
- secondary: bfloat16 [8192, 512], P('node'), may hold values from -0.0625 to 0.0625
- master: float32 [8192, 512], P(('node', 'rep')), may hold values from -0.0625 to 0.0625
- moment_first: float32 [4096, 1024], P(('node', 'rep')), may hold values from -0.09375 to 0.09375
- moment_second: float32 [4096, 1024], P(('node', 'rep')), may hold values from 6.1035156e-05 to 0.0009765625
- signs: int32 [1024], replicated, may hold values from 0 to 1
Outputs:
- keys: bfloat16 [4096, 512], P(('node', 'rep'))
- token_grad: bfloat16 [4096, 8192], P(('node', 'rep'))
- new_master: float32 [8192, 512], P(('node', 'rep'))
- new_first: float32 [4096, 1024], P(('node', 'rep'))
- new_second: float32 [4096, 1024], P(('node', 'rep'))
- new_secondary: bfloat16 [8192, 512], P('node')
The draws below stay inside these ranges and needn't reach their ends.
All inputs are finite; a program needn't handle non-finite values.
Results may differ from the reference program's by a relative error of at most 0.0049.
Values may be sent and summed in bfloat16 or wider, within the bound.
A program may use at most 128 MiB of HBM per device.

```python
import math
import jax
import jax.numpy as jnp
from jax import lax

D = 8192
KV = 512
TOK_DEV = 128
PAIR_GAP = 16
TOKENS = 4096
N_NODE = 8
N_REP = 4


def with_ends(entries, own_key, low, high):
    longest = entries.shape.index(max(entries.shape))
    spots = []
    for shift in (0, 1):
        where = [jax.random.randint(jax.random.fold_in(own_key, axis), (), 0, length) for axis, length in enumerate(entries.shape)]
        where[longest] = (where[longest] + shift) % entries.shape[longest]
        spots.append(tuple(where))
    return entries.at[spots[0]].set(low).at[spots[1]].set(high)


def strengthened(drawn, key, source, target, blocks, factor):
    def block_of(dim):
        return (jnp.arange(drawn.shape[dim]) // (drawn.shape[dim] // blocks)).reshape((-1,) + (1,) * (drawn.ndim - 1 - dim))

    near = jax.random.permutation(key, blocks)[block_of(target)]
    second = (block_of(target) + blocks // 2) % blocks
    return jnp.where((block_of(source) == near) | (block_of(source) == second), factor * drawn, drawn)


def block_scale(key, dims, split, low, largest):
    gain = 1.0
    for axis_at, blocks in split:
        draws = jax.random.uniform(jax.random.fold_in(jax.random.fold_in(key, 6), axis_at), (blocks,), jnp.float32, low / len(split), largest / len(split))
        gain = gain * jnp.repeat(jnp.exp(draws), dims[axis_at] // blocks).reshape((-1,) + (1,) * (len(dims) - 1 - axis_at))
    return gain


def normal_values(own_key, dims, deviation, limit, pieces=(), kind=jnp.bfloat16):
    drawn = deviation * jax.random.normal(own_key, dims, jnp.float32)
    if pieces:
        drawn = drawn * block_scale(own_key, dims, pieces, -0.22, 0.18)
    return jnp.clip(drawn, -limit, limit).astype(kind)


def heavy_noise(key, shape, deviation, bound, shards, heavy, kind=jnp.bfloat16):
    array = deviation * jax.random.normal(key, shape, jnp.float32)
    if shards:
        array = array * block_scale(key, shape, shards, -0.22, 0.18)
    return jnp.clip(strengthened(array, jax.random.fold_in(key, 3), *heavy), -bound, bound).astype(kind)


def setup_inputs(seed: int = 0) -> dict:
    key_of = jax.random.split(jax.random.key(seed), 9)
    tokens = heavy_noise(key_of[0], (TOKENS, D), 1.0, 6.0, ((0, 32),), (0, 1, 32, 2.75))
    norm_gain = jnp.clip(1.0 + 0.1 * jax.random.normal(key_of[1], (D,), jnp.float32), 0.5, 1.5)
    key_cotangent = normal_values(key_of[2], (TOKENS, KV), 1.0, 6.0, ((0, 32),))
    secondary = normal_values(key_of[3], (D, KV), D ** -0.5, 0.0625, ((0, 8),))
    master = normal_values(key_of[4], (D, KV), D ** -0.5, 0.0625, ((0, 32),), jnp.float32)
    moment_first = normal_values(key_of[5], (D // 2, 2 * KV), (1.0 / (TOK_DEV * N_NODE * N_REP) ** 0.5), 0.09375, ((0, 32),), jnp.float32)
    moment_second = jnp.clip(jnp.exp(math.log(0.0009765625) - 2.7725887 * jax.random.uniform(key_of[6], (D // 2, 2 * KV), jnp.float32) ** block_scale(key_of[6], (D // 2, 2 * KV), ((0, 32),), -0.2, 0.2)), 6.103515625e-05, 0.0009765625)
    signs = with_ends(jax.random.randint(key_of[7], (2 * KV,), 0, 2), jax.random.fold_in(key_of[7], 1), 0, 1).astype(jnp.int32)
    return dict(tokens=tokens, norm_gain=norm_gain, key_cotangent=key_cotangent, secondary=secondary, master=master, moment_first=moment_first, moment_second=moment_second, signs=signs)


norm_eps = 1e-05
adam_eps = 1e-08
beta_first = 0.9
beta_second = 0.95
adam_steps = 10
learn_rate = 0.002
weight_decay = 0.1

def sylvester(extent):
    position = jnp.arange(extent, dtype=jnp.int32)
    parity = jnp.zeros((extent, extent), jnp.int32)
    for bit_place in range(extent.bit_length() - 1):
        parity = parity + (position[:, None] >> bit_place & 1) * (position[None, :] >> bit_place & 1)
    return (1 - 2 * (parity % 2)).astype(jnp.float32)

def reference(tokens, norm_gain, key_cotangent, secondary, master, moment_first, moment_second, signs):
    devices = N_NODE * N_REP
    had_table = sylvester(KV)
    sign_rows = (1 - 2 * signs).astype(jnp.float32).reshape(2, KV)
    rot_scale = 1.0 / (math.sqrt(2 * KV) * TOK_DEV * devices)
    token_blocks = tokens.reshape(devices, TOK_DEV, D)
    cot_blocks = key_cotangent.reshape(devices, TOK_DEV, KV)

    def device_step(running, block):
        activations, cotangent = block
        floats = activations.astype(jnp.float32)
        inverse = lax.rsqrt(lax.optimization_barrier(jnp.mean(floats * floats, axis=-1, keepdims=True)) + norm_eps)
        normed = floats * inverse
        hidden = (normed * norm_gain).astype(jnp.bfloat16)
        keys = jnp.dot(hidden, secondary, preferred_element_type=jnp.float32).astype(jnp.bfloat16)
        hidden_grad = jnp.dot(cotangent, secondary.T, preferred_element_type=jnp.float32)
        scaled = hidden_grad * norm_gain
        token_grad = (inverse * (scaled - normed * lax.optimization_barrier(jnp.mean(scaled * normed, axis=-1, keepdims=True)))).astype(jnp.bfloat16)
        flipped = cotangent.astype(jnp.float32)[:, None, :] * sign_rows
        rotated = (jnp.einsum('tak,kl->tal', flipped, had_table, precision=lax.Precision.HIGHEST) * rot_scale).astype(jnp.bfloat16)
        grouped = hidden.reshape(TOK_DEV, D // (2 * PAIR_GAP), 2, PAIR_GAP).astype(jnp.float32)
        halves = jnp.einsum('tgaj,tak->agjk', grouped, rotated.astype(jnp.float32), precision=lax.Precision.HIGHEST)
        term = jnp.concatenate([halves[0] + halves[1], halves[0] - halves[1]], axis=-1).reshape(D // 2, 2 * KV)
        coded_term = lax.optimization_barrier(term.astype(jnp.bfloat16)).astype(jnp.float32)
        return (running + coded_term, (keys, token_grad))
    start_sum = jnp.zeros((D // 2, 2 * KV), jnp.float32)
    coded, (all_keys, all_grads) = lax.scan(device_step, start_sum, (token_blocks, cot_blocks))
    new_first = beta_first * moment_first + (1.0 - beta_first) * coded
    new_second = beta_second * moment_second + (1.0 - beta_second) * coded * coded
    first_hat = new_first / (1.0 - beta_first ** adam_steps)
    second_hat = new_second / (1.0 - beta_second ** adam_steps)
    ratio = first_hat / (jnp.sqrt(second_hat) + adam_eps)
    lower = ratio[:, :KV]
    upper = ratio[:, KV:]
    norm_root = math.sqrt(2 * KV)
    row_even = jnp.dot(lower + upper, had_table, precision=lax.Precision.HIGHEST) / norm_root * sign_rows[0]
    row_odd = jnp.dot(lower - upper, had_table, precision=lax.Precision.HIGHEST) / norm_root * sign_rows[1]
    stacked = jnp.stack([row_even, row_odd], axis=1)
    update = stacked.reshape(D // (2 * PAIR_GAP), PAIR_GAP, 2, KV).transpose(0, 2, 1, 3).reshape(D, KV)
    new_master = master - learn_rate * (update + weight_decay * master)
    keys_out = all_keys.reshape(devices * TOK_DEV, KV)
    grads_out = all_grads.reshape(devices * TOK_DEV, D)
    return (keys_out, grads_out, new_master, new_first, new_second, new_master.astype(jnp.bfloat16))
```

```python
import functools
import math

import jax
import jax.numpy as jnp
from jax import lax
from jax.experimental import pallas as pl
from jax.experimental.pallas import tpu as pltpu
from jax.sharding import PartitionSpec as P

PAIR_GAP = 16
MESH = pl.DeviceIdType.MESH

norm_eps = 1e-05
adam_eps = 1e-08
beta_first = 0.9
beta_second = 0.95
adam_steps = 10
learn_rate = 0.002
weight_decay = 0.1

ANY = pl.BlockSpec(memory_space=pl.ANY)
VMEM = pl.BlockSpec(memory_space=pltpu.VMEM)


def sylvester(extent):
    position = jnp.arange(extent, dtype=jnp.int32)
    parity = jnp.zeros((extent, extent), jnp.int32)
    for bit_place in range(extent.bit_length() - 1):
        parity = parity + (position[:, None] >> bit_place & 1) * (
            position[None, :] >> bit_place & 1
        )
    return (1 - 2 * (parity % 2)).astype(jnp.float32)


def split(index):
    return index // 2, lax.rem(index, 2)


def greet(peers):
    barrier = pltpu.get_barrier_semaphore()
    for peer in peers:
        pl.semaphore_signal(barrier, inc=1, device_id=peer, device_id_type=MESH)
    pl.semaphore_wait(barrier, len(peers))


def remote(src, dst, send, recv, peer):
    return pltpu.make_async_remote_copy(
        src_ref=src,
        dst_ref=dst,
        send_sem=send,
        recv_sem=recv,
        device_id=peer,
        device_id_type=MESH,
    )


def axis_peers(axis, size):
    me = lax.axis_index(axis)
    return [{axis: lax.rem(me + k, size)} for k in range(1, size)]


def pair_peers(axis, size):
    high, low = split(lax.axis_index(axis))
    half = size // 2
    partner = {axis: high * 2 + 1 - low}
    same = [{axis: lax.rem(high + k, half) * 2 + low} for k in range(1, half)]
    return partner, same


class PairGather:
    def __init__(self, axis, size, src, out, local_sem, send, recv):
        self.half = size // 2
        me = lax.axis_index(axis)
        high, low = split(me)
        partner, same = pair_peers(axis, size)
        self.local = pltpu.make_async_copy(src, out.at[me], local_sem)
        self.first = [
            remote(src, out.at[me], send.at[0, k], recv.at[0, k], same[k - 1])
            for k in range(1, self.half)
        ]
        self.second = [remote(src, out.at[me], send.at[1, 0], recv.at[1, 0], partner)]
        for k in range(1, self.half):
            origin = lax.rem(high + self.half - k, self.half) * 2 + low
            self.second.append(
                remote(out.at[origin], out.at[origin], send.at[1, k], recv.at[1, k], partner)
            )

    def start(self):
        for copy in self.first:
            copy.start()
        self.second[0].start()
        self.local.start()

    def forward(self):
        for arrived, onward in zip(self.first, self.second[1:]):
            arrived.wait_recv()
            onward.start()

    def finish(self):
        for copy in self.second:
            copy.wait_recv()
        for copy in self.first + self.second:
            copy.wait_send()
        self.local.wait()


def gather_kernel(
    nodes, reps, hid, cot, sec, hid_out, cot_out, sec_out, hs, hr, cs, cr, ss, sr, local
):
    rep = lax.axis_index("rep")
    partner, same = pair_peers("node", nodes)
    rep_peers = axis_peers("rep", reps)
    greet(rep_peers + [partner] + same)
    own = [
        pltpu.make_async_copy(hid.at[rep], hid_out.at[rep], local.at[0]),
        pltpu.make_async_copy(cot, cot_out.at[rep], local.at[1]),
    ]
    rows = sec_out.shape[1]
    weights = PairGather(
        "node", nodes, sec.at[pl.ds(pl.multiple_of(rep * rows, rows), rows)], sec_out,
        local.at[2], ss, sr,
    )
    weights.start()
    moves = []
    for k, peer in enumerate(rep_peers):
        moves.append(remote(cot, cot_out.at[rep], cs.at[k], cr.at[k], peer))
    for k, peer in enumerate(rep_peers):
        moves.append(remote(hid.at[peer["rep"]], hid_out.at[rep], hs.at[k], hr.at[k], peer))
    for copy in moves + own:
        copy.start()
    weights.forward()
    for copy in moves:
        copy.wait()
    weights.finish()
    for copy in own:
        copy.wait()


def gather(nodes, reps, hid, cot, sec):
    rows = sec.shape[0] // reps
    dma = pltpu.SemaphoreType.DMA
    return pl.pallas_call(
        functools.partial(gather_kernel, nodes, reps),
        out_shape=(
            jax.ShapeDtypeStruct(hid.shape, hid.dtype),
            jax.ShapeDtypeStruct((reps,) + cot.shape, cot.dtype),
            jax.ShapeDtypeStruct((nodes, rows, sec.shape[1]), sec.dtype),
        ),
        in_specs=[ANY] * 3,
        out_specs=(VMEM,) * 3,
        scratch_shapes=[dma((reps - 1,))] * 4 + [dma((2, nodes // 2))] * 2 + [dma((3,))],
        compiler_params=pltpu.CompilerParams(collective_id=0, has_side_effects=True),
    )(hid, cot, sec)


def reduce_kernel(
    nodes, reps, term, part, grad, coded, keys, grad_out,
    from_pair, to_same, from_same, key_in, ps, pr, zs, zr, ks, kr, gs, gr, local,
):
    rep = lax.axis_index("rep")
    high, low = split(lax.axis_index("node"))
    half = nodes // 2
    partner, same = pair_peers("node", nodes)
    rep_peers = axis_peers("rep", reps)
    greet(rep_peers + [partner] + same)
    f32 = jnp.float32
    pair = {}
    for k in list(range(1, half)) + [0]:
        there = lax.rem(high + k, half)
        pair[k] = remote(
            term.at[there * 2 + 1 - low], from_pair.at[k], ps.at[k], pr.at[k], partner
        )
        pair[k].start()
    swaps = []
    for k, peer in enumerate(rep_peers):
        swaps.append(remote(part.at[peer["rep"]], key_in.at[k], ks.at[k], kr.at[k], peer))
    for k, peer in enumerate(rep_peers):
        swaps.append(remote(grad.at[peer["rep"]], grad_out.at[rep], gs.at[k], gr.at[k], peer))
    own = pltpu.make_async_copy(grad.at[rep], grad_out.at[rep], local.at[0])
    for copy in swaps + [own]:
        copy.start()
    onward = []
    for k in range(1, half):
        there = lax.rem(high + k, half)
        pair[k].wait_recv()
        to_same[k - 1] = (
            term[there * 2 + low].astype(f32) + from_pair[k].astype(f32)
        ).astype(to_same.dtype)
        onward.append(
            remote(
                to_same.at[k - 1], from_same.at[k - 1], zs.at[k - 1], zr.at[k - 1], same[k - 1]
            )
        )
        onward[-1].start()
    pair[0].wait_recv()
    coded[...] = term[high * 2 + low].astype(f32) + from_pair[0].astype(f32)
    for k in range(reps - 1):
        swaps[k].wait_recv()
    total = part[rep].astype(f32)
    for k in range(reps - 1):
        total = total + key_in[k].astype(f32)
    keys[...] = total.astype(keys.dtype)
    for k in range(1, half):
        onward[k - 1].wait_recv()
        coded[...] += from_same[k - 1].astype(f32)
    for copy in swaps[reps - 1 :]:
        copy.wait_recv()
    for copy in swaps + onward + list(pair.values()):
        copy.wait_send()
    own.wait()


def reduce(nodes, reps, term, part, grad):
    dma = pltpu.SemaphoreType.DMA
    half = nodes // 2
    block = term.shape[1:]
    return pl.pallas_call(
        functools.partial(reduce_kernel, nodes, reps),
        out_shape=(
            jax.ShapeDtypeStruct(block, jnp.float32),
            jax.ShapeDtypeStruct(part.shape[1:], part.dtype),
            jax.ShapeDtypeStruct(grad.shape, grad.dtype),
        ),
        in_specs=[VMEM, VMEM, ANY],
        out_specs=(VMEM,) * 3,
        scratch_shapes=[
            pltpu.VMEM((half,) + block, term.dtype),
            pltpu.VMEM((half - 1,) + block, term.dtype),
            pltpu.VMEM((half - 1,) + block, term.dtype),
            pltpu.VMEM((reps - 1,) + part.shape[1:], part.dtype),
        ]
        + [dma((half,))] * 2
        + [dma((half - 1,))] * 2
        + [dma((reps - 1,))] * 4
        + [dma((1,))],
        compiler_params=pltpu.CompilerParams(collective_id=1, has_side_effects=True),
    )(term, part, grad)


def spread_kernel(reps, src, out, send, recv, local):
    partner, same = pair_peers("rep", reps)
    greet([partner] + same)
    rows = PairGather("rep", reps, src, out, local.at[0], send, recv)
    rows.start()
    rows.forward()
    rows.finish()


def spread(reps, rows):
    dma = pltpu.SemaphoreType.DMA
    return pl.pallas_call(
        functools.partial(spread_kernel, reps),
        out_shape=jax.ShapeDtypeStruct((reps,) + rows.shape, rows.dtype),
        in_specs=[VMEM],
        out_specs=VMEM,
        scratch_shapes=[dma((2, reps // 2))] * 2 + [dma((1,))],
        compiler_params=pltpu.CompilerParams(collective_id=2, has_side_effects=True),
    )(rows)


def shards(tokens, norm_gain, key_cotangent, secondary, master, moment_first, moment_second, signs):
    tok_rows, model_width = tokens.shape
    key_width = key_cotangent.shape[1]
    nodes = lax.axis_size("node")
    reps = lax.axis_size("rep")
    all_tokens = tok_rows * nodes * reps
    group_tokens = tok_rows * reps
    master_rows = master.shape[0]
    quarter = model_width // reps
    had_table = sylvester(key_width)
    sign_rows = (1 - 2 * signs).astype(jnp.float32).reshape(2, key_width)
    floats = tokens.astype(jnp.float32)
    inverse = lax.rsqrt(jnp.mean(floats * floats, axis=-1, keepdims=True) + norm_eps)
    normed = floats * inverse
    hidden = (normed * norm_gain).astype(jnp.bfloat16)
    outgoing = (
        hidden.reshape(tok_rows, nodes, reps, master_rows)
        .transpose(2, 0, 1, 3)
        .reshape(reps, tok_rows, quarter)
    )
    hid, cot, sec = gather(nodes, reps, outgoing, key_cotangent, secondary)
    hid = hid.reshape(group_tokens, quarter)
    cot = cot.reshape(group_tokens, key_width)
    sec = sec.reshape(quarter, key_width)
    rot_scale = 1.0 / (math.sqrt(2 * key_width) * all_tokens)
    table = (sign_rows[:, :, None] * had_table).astype(jnp.bfloat16)
    table = jnp.concatenate([table[0], table[1]], axis=1)
    rotated = (jnp.dot(cot, table, preferred_element_type=jnp.float32) * rot_scale).astype(
        jnp.bfloat16
    )
    products = lax.dot_general(
        hid, rotated, (((0,), (0,)), ((), ())), preferred_element_type=jnp.float32
    ).reshape(quarter // (2 * PAIR_GAP), 2, PAIR_GAP, 2 * key_width)
    upper_rows = products[:, 0, :, :key_width]
    lower_rows = products[:, 1, :, key_width:]
    term = jnp.concatenate([upper_rows + lower_rows, upper_rows - lower_rows], axis=-1)
    term = term.astype(jnp.bfloat16).reshape(nodes, master_rows // 2, 2 * key_width)
    part = jnp.dot(hid, sec, preferred_element_type=jnp.float32).astype(jnp.bfloat16)
    grad = lax.dot_general(
        cot, sec, (((1,), (1,)), ((), ())), preferred_element_type=jnp.float32
    ).astype(jnp.bfloat16)
    coded, keys, hidden_grad = reduce(
        nodes,
        reps,
        term,
        part.reshape(reps, tok_rows, key_width),
        grad.reshape(reps, tok_rows, quarter),
    )
    new_first = beta_first * moment_first + (1.0 - beta_first) * coded
    new_second = beta_second * moment_second + (1.0 - beta_second) * coded * coded
    first_hat = new_first / (1.0 - beta_first**adam_steps)
    second_hat = new_second / (1.0 - beta_second**adam_steps)
    ratio = first_hat / (jnp.sqrt(second_hat) + adam_eps)
    lower = ratio[:, :key_width]
    upper = ratio[:, key_width:]
    norm_root = math.sqrt(2 * key_width)
    row_even = (
        jnp.dot(lower + upper, had_table, precision=lax.Precision.HIGHEST)
        / norm_root
        * sign_rows[0]
    )
    row_odd = (
        jnp.dot(lower - upper, had_table, precision=lax.Precision.HIGHEST)
        / norm_root
        * sign_rows[1]
    )
    groups = master_rows // (2 * PAIR_GAP)
    update = jnp.stack(
        [
            row_even.reshape(groups, PAIR_GAP, key_width),
            row_odd.reshape(groups, PAIR_GAP, key_width),
        ],
        axis=1,
    ).reshape(master_rows, key_width)
    new_master = master - learn_rate * (update + weight_decay * master)
    new_secondary = spread(reps, new_master.astype(jnp.bfloat16)).reshape(
        reps * master_rows, key_width
    )
    hidden_grad = (
        hidden_grad.reshape(reps, tok_rows, nodes, master_rows)
        .transpose(1, 2, 0, 3)
        .reshape(tok_rows, model_width)
        .astype(jnp.float32)
    )
    scaled = hidden_grad * norm_gain
    token_grad = (
        inverse * (scaled - normed * jnp.mean(scaled * normed, axis=-1, keepdims=True))
    ).astype(jnp.bfloat16)
    return (keys, token_grad, new_master, new_first, new_second, new_secondary)


def solution(mesh):
    return jax.shard_map(
        shards,
        mesh=mesh,
        in_specs=(
            P(("node", "rep"), None),
            P(),
            P(("node", "rep"), None),
            P("node", None),
            P(("node", "rep"), None),
            P(("node", "rep"), None),
            P(("node", "rep"), None),
            P(),
        ),
        out_specs=(
            P(("node", "rep"), None),
            P(("node", "rep"), None),
            P(("node", "rep"), None),
            P(("node", "rep"), None),
            P(("node", "rep"), None),
            P("node", None),
        ),
        check_vma=False,
    )
```

```python
import functools
import math

import jax
import jax.numpy as jnp
from jax import lax
from jax.experimental import pallas as pl
from jax.experimental.pallas import tpu as pltpu
from jax.sharding import PartitionSpec as P

PAIR_GAP = 16
MESH = pl.DeviceIdType.MESH

norm_eps = 1e-05
adam_eps = 1e-08
beta_first = 0.9
beta_second = 0.95
adam_steps = 10
learn_rate = 0.002
weight_decay = 0.1

ANY = pl.BlockSpec(memory_space=pl.ANY)
VMEM = pl.BlockSpec(memory_space=pltpu.VMEM)


def sylvester(extent):
    position = jnp.arange(extent, dtype=jnp.int32)
    parity = jnp.zeros((extent, extent), jnp.int32)
    for bit_place in range(extent.bit_length() - 1):
        parity = parity + (position[:, None] >> bit_place & 1) * (
            position[None, :] >> bit_place & 1
        )
    return (1 - 2 * (parity % 2)).astype(jnp.float32)


def split(index):
    return index // 2, lax.rem(index, 2)


def greet(peers):
    barrier = pltpu.get_barrier_semaphore()
    for peer in peers:
        pl.semaphore_signal(barrier, inc=1, device_id=peer, device_id_type=MESH)
    pl.semaphore_wait(barrier, len(peers))


def remote(src, dst, send, recv, peer):
    return pltpu.make_async_remote_copy(
        src_ref=src,
        dst_ref=dst,
        send_sem=send,
        recv_sem=recv,
        device_id=peer,
        device_id_type=MESH,
    )


def axis_peers(axis, size):
    me = lax.axis_index(axis)
    return [{axis: lax.rem(me + k, size)} for k in range(1, size)]


def pair_peers(axis, size):
    high, low = split(lax.axis_index(axis))
    half = size // 2
    partner = {axis: high * 2 + 1 - low}
    same = [{axis: lax.rem(high + k, half) * 2 + low} for k in range(1, half)]
    return partner, same


class PairGather:
    def __init__(self, axis, size, src, out, local_sem, send, recv):
        self.half = size // 2
        me = lax.axis_index(axis)
        high, low = split(me)
        partner, same = pair_peers(axis, size)
        self.local = pltpu.make_async_copy(src, out.at[me], local_sem)
        self.first = [
            remote(src, out.at[me], send.at[0, k], recv.at[0, k], same[k - 1])
            for k in range(1, self.half)
        ]
        self.second = [remote(src, out.at[me], send.at[1, 0], recv.at[1, 0], partner)]
        for k in range(1, self.half):
            origin = lax.rem(high + self.half - k, self.half) * 2 + low
            self.second.append(
                remote(out.at[origin], out.at[origin], send.at[1, k], recv.at[1, k], partner)
            )

    def start(self):
        for copy in self.first:
            copy.start()
        self.second[0].start()
        self.local.start()

    def forward(self, k):
        self.first[k - 1].wait_recv()
        self.second[k].start()

    def finish(self):
        for copy in self.second:
            copy.wait_recv()
        for copy in self.first + self.second:
            copy.wait_send()
        self.local.wait()


def step_kernel(
    nodes, reps, aligned, scale, hid, cot, sec, table, coded, keys, grad_out,
    hid_in, cot_in, sec_in, rot, term, grad, acc, part,
    from_pair, to_same, from_same, key_in,
    cs, cr, hs, hr, ss, sr, ps, pr, zs, zr, gs, gr, ks, kr, cot_own, hid_own, sec_own, grad_own,
):
    f32 = jnp.float32
    rep = lax.axis_index("rep")
    high, low = split(lax.axis_index("node"))
    half = nodes // 2
    partner, same = pair_peers("node", nodes)
    rep_peers = axis_peers("rep", reps)
    columns, key_width = sec_in.shape[1:]
    tok_rows = cot_in.shape[1]
    group_tokens = reps * tok_rows

    def piece(ref, node, owner):
        index = node * reps + owner
        if aligned:
            return ref.at[:, pl.ds(pl.multiple_of(index * columns, columns), columns)]
        return ref.at[index]

    greet(rep_peers + [partner] + same)
    weights = PairGather(
        "node", nodes, sec.at[pl.ds(pl.multiple_of(rep * columns, columns), columns)], sec_in,
        sec_own.at[0], ss, sr,
    )
    weights.start()
    cot_moves = [
        remote(cot, cot_in.at[rep], cs.at[k], cr.at[k], peer) for k, peer in enumerate(rep_peers)
    ]
    cot_moves.append(pltpu.make_async_copy(cot, cot_in.at[rep], cot_own.at[0]))
    for copy in cot_moves:
        copy.start()
    turns = list(range(1, half)) + [0]
    order = [lax.rem(high + k, half) * 2 + 1 - low for k in turns]
    order += [lax.rem(high + k, half) * 2 + low for k in turns]
    hid_moves = []
    for i, node in enumerate(order):
        moves = [
            remote(
                piece(hid, node, peer["rep"]), hid_in.at[node, rep], hs.at[k, i], hr.at[k, i], peer
            )
            for k, peer in enumerate(rep_peers)
        ]
        moves.append(
            pltpu.make_async_copy(piece(hid, node, rep), hid_in.at[node, rep], hid_own.at[i])
        )
        for copy in moves:
            copy.start()
        hid_moves.append(moves)

    for copy in cot_moves:
        copy.wait()
    group_cot = cot_in[...].reshape(group_tokens, key_width)
    rot[...] = (jnp.dot(group_cot, table[...], preferred_element_type=f32) * scale).astype(
        rot.dtype
    )
    acc[...] = jnp.zeros_like(acc)

    def make_term(i):
        for copy in hid_moves[i]:
            copy.wait()
        chunk = hid_in[order[i]].reshape(group_tokens, columns)
        product = lax.dot_general(
            chunk, rot[...], (((0,), (0,)), ((), ())), preferred_element_type=f32
        ).reshape(columns // (2 * PAIR_GAP), 2, PAIR_GAP, 2 * key_width)
        first = product[:, 0, :, :key_width].reshape(columns // 2, key_width)
        second = product[:, 1, :, key_width:].reshape(columns // 2, key_width)
        term[i, :, :key_width] = (first + second).astype(term.dtype)
        term[i, :, key_width:] = (first - second).astype(term.dtype)

    swaps = []
    stays = []

    def use_weights(count, node):
        block = sec_in[node]
        rows = lax.dot_general(
            cot_in[...].reshape(group_tokens, key_width), block, (((1,), (1,)), ((), ())),
            preferred_element_type=f32,
        )
        grad[node] = rows.astype(grad.dtype).reshape(reps, tok_rows, columns)
        for k, peer in enumerate(rep_peers):
            copy = remote(
                grad.at[node, peer["rep"]], piece(grad_out, node, rep),
                gs.at[k, count], gr.at[k, count], peer,
            )
            copy.start()
            swaps.append(copy)
        copy = pltpu.make_async_copy(
            grad.at[node, rep], piece(grad_out, node, rep), grad_own.at[count]
        )
        copy.start()
        stays.append(copy)
        chunk = hid_in[node].reshape(group_tokens, columns)
        acc[...] += jnp.dot(chunk, block, preferred_element_type=f32)

    pairs = []
    for i in range(half):
        make_term(i)
        pairs.append(remote(term.at[i], from_pair.at[i], ps.at[i], pr.at[i], partner))
        pairs[-1].start()
        if i:
            weights.forward(i)
    weights.local.wait()
    onward = []
    for j, k in enumerate(turns):
        make_term(half + j)
        pairs[j].wait_recv()
        total = term[half + j].astype(f32) + from_pair[j].astype(f32)
        if k:
            to_same[j] = total.astype(to_same.dtype)
            onward.append(remote(to_same.at[j], from_same.at[j], zs.at[j], zr.at[j], same[k - 1]))
            onward[-1].start()
        else:
            coded[...] = total
        use_weights(j, order[half + j])
    for j in range(half):
        weights.second[j].wait_recv()
        use_weights(half + j, lax.rem(high + half - j, half) * 2 + 1 - low)
    part[...] = acc[...].astype(part.dtype).reshape(part.shape)
    key_moves = [
        remote(part.at[peer["rep"]], key_in.at[k], ks.at[k], kr.at[k], peer)
        for k, peer in enumerate(rep_peers)
    ]
    for copy in key_moves:
        copy.start()
    for j, copy in enumerate(onward):
        copy.wait_recv()
        coded[...] += from_same[j].astype(f32)
    total = part[rep].astype(f32)
    for k, copy in enumerate(key_moves):
        copy.wait_recv()
        total = total + key_in[k].astype(f32)
    keys[...] = total.astype(keys.dtype)
    for copy in swaps:
        copy.wait()
    for copy in stays:
        copy.wait()
    for copy in weights.first + weights.second + pairs + onward + key_moves:
        copy.wait_send()


def step(nodes, reps, aligned, scale, hid, cot, sec, table):
    dma = pltpu.SemaphoreType.DMA
    half = nodes // 2
    columns = sec.shape[0] // reps
    tok_rows, key_width = cot.shape
    group_tokens = reps * tok_rows
    block = (columns // 2, 2 * key_width)
    bf16 = jnp.bfloat16
    return pl.pallas_call(
        functools.partial(step_kernel, nodes, reps, aligned, scale),
        out_shape=(
            jax.ShapeDtypeStruct(block, jnp.float32),
            jax.ShapeDtypeStruct(cot.shape, bf16),
            jax.ShapeDtypeStruct(hid.shape, bf16),
        ),
        in_specs=[ANY, ANY, ANY, VMEM],
        out_specs=(VMEM,) * 3,
        scratch_shapes=[
            pltpu.VMEM((nodes, reps, tok_rows, columns), bf16),
            pltpu.VMEM((reps, tok_rows, key_width), bf16),
            pltpu.VMEM((nodes, columns, key_width), bf16),
            pltpu.VMEM((group_tokens, 2 * key_width), bf16),
            pltpu.VMEM((nodes,) + block, bf16),
            pltpu.VMEM((nodes, reps, tok_rows, columns), bf16),
            pltpu.VMEM((group_tokens, key_width), jnp.float32),
            pltpu.VMEM((reps, tok_rows, key_width), bf16),
            pltpu.VMEM((half,) + block, bf16),
            pltpu.VMEM((half - 1,) + block, bf16),
            pltpu.VMEM((half - 1,) + block, bf16),
            pltpu.VMEM((reps - 1, tok_rows, key_width), bf16),
        ]
        + [dma((reps - 1,))] * 2
        + [dma((reps - 1, nodes))] * 2
        + [dma((2, half))] * 2
        + [dma((half,))] * 2
        + [dma((half - 1,))] * 2
        + [dma((reps - 1, nodes))] * 2
        + [dma((reps - 1,))] * 2
        + [dma((1,)), dma((nodes,)), dma((1,)), dma((nodes,))],
        compiler_params=pltpu.CompilerParams(collective_id=0, has_side_effects=True),
    )(hid, cot, sec, table)


def spread_kernel(reps, src, out, send, recv, local):
    partner, same = pair_peers("rep", reps)
    greet([partner] + same)
    rows = PairGather("rep", reps, src, out, local.at[0], send, recv)
    rows.start()
    for k in range(1, reps // 2):
        rows.forward(k)
    rows.finish()


def spread(reps, rows):
    dma = pltpu.SemaphoreType.DMA
    return pl.pallas_call(
        functools.partial(spread_kernel, reps),
        out_shape=jax.ShapeDtypeStruct((reps,) + rows.shape, rows.dtype),
        in_specs=[VMEM],
        out_specs=VMEM,
        scratch_shapes=[dma((2, reps // 2))] * 2 + [dma((1,))],
        compiler_params=pltpu.CompilerParams(collective_id=1, has_side_effects=True),
    )(rows)


def shards(tokens, norm_gain, key_cotangent, secondary, master, moment_first, moment_second, signs):
    tok_rows, model_width = tokens.shape
    key_width = key_cotangent.shape[1]
    nodes = lax.axis_size("node")
    reps = lax.axis_size("rep")
    all_tokens = tok_rows * nodes * reps
    master_rows = master.shape[0]
    had_table = sylvester(key_width)
    sign_rows = (1 - 2 * signs).astype(jnp.float32).reshape(2, key_width)
    floats = tokens.astype(jnp.float32)
    inverse = lax.rsqrt(jnp.mean(floats * floats, axis=-1, keepdims=True) + norm_eps)
    normed = floats * inverse
    hidden = (normed * norm_gain).astype(jnp.bfloat16)
    aligned = master_rows % 128 == 0
    if not aligned:
        hidden = hidden.reshape(tok_rows, nodes * reps, master_rows).transpose(1, 0, 2)
    rot_scale = 1.0 / (math.sqrt(2 * key_width) * all_tokens)
    table = (had_table[:, None, :] * sign_rows.T[:, :, None]).astype(jnp.bfloat16)
    coded, keys, hidden_grad = step(
        nodes, reps, aligned, rot_scale, hidden, key_cotangent, secondary,
        table.reshape(key_width, 2 * key_width),
    )
    if not aligned:
        hidden_grad = hidden_grad.transpose(1, 0, 2).reshape(tok_rows, model_width)
    hidden_grad = hidden_grad.astype(jnp.float32)
    new_first = beta_first * moment_first + (1.0 - beta_first) * coded
    new_second = beta_second * moment_second + (1.0 - beta_second) * coded * coded
    first_hat = new_first / (1.0 - beta_first**adam_steps)
    second_hat = new_second / (1.0 - beta_second**adam_steps)
    ratio = first_hat / (jnp.sqrt(second_hat) + adam_eps)
    lower = ratio[:, :key_width]
    upper = ratio[:, key_width:]
    norm_root = math.sqrt(2 * key_width)
    row_even = (
        jnp.dot(lower + upper, had_table, precision=lax.Precision.HIGHEST)
        / norm_root
        * sign_rows[0]
    )
    row_odd = (
        jnp.dot(lower - upper, had_table, precision=lax.Precision.HIGHEST)
        / norm_root
        * sign_rows[1]
    )
    groups = master_rows // (2 * PAIR_GAP)
    update = jnp.stack(
        [
            row_even.reshape(groups, PAIR_GAP, key_width),
            row_odd.reshape(groups, PAIR_GAP, key_width),
        ],
        axis=1,
    ).reshape(master_rows, key_width)
    new_master = master - learn_rate * (update + weight_decay * master)
    new_secondary = spread(reps, new_master.astype(jnp.bfloat16)).reshape(
        reps * master_rows, key_width
    )
    scaled = hidden_grad * norm_gain
    token_grad = (
        inverse * (scaled - normed * jnp.mean(scaled * normed, axis=-1, keepdims=True))
    ).astype(jnp.bfloat16)
    return (keys, token_grad, new_master, new_first, new_second, new_secondary)


def solution(mesh):
    return jax.shard_map(
        shards,
        mesh=mesh,
        in_specs=(
            P(("node", "rep"), None),
            P(),
            P(("node", "rep"), None),
            P("node", None),
            P(("node", "rep"), None),
            P(("node", "rep"), None),
            P(("node", "rep"), None),
            P(),
        ),
        out_specs=(
            P(("node", "rep"), None),
            P(("node", "rep"), None),
            P(("node", "rep"), None),
            P(("node", "rep"), None),
            P(("node", "rep"), None),
            P("node", None),
        ),
        check_vma=False,
    )
```
